32 devices in a mesh: clip: 8 (over y, x, core), shard: 4 (over z).
Axes of the slice: x: 2, y: 2, z: 4, core: 2. Of those that a mesh axis runs over, the one named last changes fastest.
Arguments:
- tokens: bfloat16 [8, 9216, 768], P('clip', 'shard'), may hold values from -6 to 6
- scales: float32 [8, 6, 9216], P('clip', None, 'shard'), may hold values from 0.1875 to 5
- slot_params: bfloat16 [768, 128], replicated, may hold values from -2 to 2
- expand_weight: bfloat16 [64, 768, 3072], P(('clip', 'shard')), may hold values from -0.21875 to 0.21875
- expand_bias: bfloat16 [64, 3072], P(('clip', 'shard')), may hold values from -4 to 4
- reduce_weight: bfloat16 [64, 3072, 768], P(('clip', 'shard')), may hold values from -0.109375 to 0.109375
- reduce_bias: bfloat16 [64, 768], P(('clip', 'shard')), may hold values from -4 to 4
Outputs:
- mixed: bfloat16 [8, 9216, 768], P('clip', 'shard')
The draws below stay inside these ranges and needn't reach their ends.
All inputs are finite; a program needn't handle non-finite values.
Results may differ from the reference program's by a relative error of at most 0.012.
The reference program's roundings to bfloat16 on the way (of `features`, `dispatch`, `slot_inputs`, `normalized`, `hidden`, `slot_outputs` and `combine`) count: a program that leaves them out, or rounds other values in their place, can miss the bound.
Values may be sent and summed in bfloat16 or wider, within the bound.
A program may use at most 128 MiB of HBM per device.

```python
import math
import jax
import jax.numpy as jnp
from jax import lax

D = 768
FF = 3072
SLOTS = 2
BLOCK = 128
EXPERTS = 64
SLOTS_ALL = 128
CLIPS = 8
LENGTH = 9216
BLOCKS = 6


def draw_tokens(key, part):
    array_shape = (CLIPS, LENGTH, D)
    values = jax.random.truncated_normal(jax.random.fold_in(key, 1), -6.0, 6.0, array_shape, jnp.float32)
    return values.astype(jnp.bfloat16)


def draw_scales(key, part):
    array_shape = (CLIPS, BLOCKS, LENGTH)
    spread = jax.random.uniform(jax.random.fold_in(key, 3), array_shape, jnp.float32, math.log(0.25), math.log(4.0))
    ramp = 0.75 + 0.5 * jnp.arange(LENGTH, dtype=jnp.float32) / LENGTH
    values = jnp.exp(spread) * ramp
    return values


def draw_slot_params(key, part):
    array_shape = (D, SLOTS_ALL)
    values = jax.random.truncated_normal(jax.random.fold_in(key, 4), -6.0, 6.0, array_shape, jnp.float32) * (0.9 / math.sqrt(D))
    return values.astype(jnp.bfloat16)


def level_of(key, extent, shards, smallest, top_value):
    gain = 1.0
    for position, parts in shards:
        steps = jax.random.uniform(jax.random.fold_in(jax.random.fold_in(key, 6), position), (parts,), jnp.float32, smallest / len(shards), top_value / len(shards))
        gain = gain * jnp.repeat(jnp.exp(steps), extent[position] // parts).reshape((-1,) + (1,) * (len(extent) - 1 - position))
    return gain


def scatter_about(own_key, dims, width, reach, shards=(), kind=jnp.bfloat16):
    values = width * jax.random.normal(own_key, dims, jnp.float32)
    if shards:
        values = values * level_of(own_key, dims, shards, -0.22, 0.18)
    return jnp.clip(values, -reach, reach).astype(kind)


def setup_inputs(seed: int = 0) -> dict:
    streams_of = jax.random.split(jax.random.key(seed), 8)
    return {
        "tokens": draw_tokens(jax.random.fold_in(streams_of[7], 71), 0),
        "scales": draw_scales(jax.random.fold_in(streams_of[7], 71), 0),
        "slot_params": draw_slot_params(jax.random.fold_in(streams_of[7], 71), 0),
        "expand_weight": scatter_about(streams_of[3], (EXPERTS, D, FF), D ** -0.5, 0.21875, ((0, 32),)),
        "expand_bias": scatter_about(streams_of[4], (EXPERTS, FF), 1.0, 4.0, ((0, 32),)),
        "reduce_weight": scatter_about(streams_of[5], (EXPERTS, FF, D), FF ** -0.5, 0.109375, ((0, 32),)),
        "reduce_bias": scatter_about(streams_of[6], (EXPERTS, D), 1.0, 4.0, ((0, 32),)),
    }


def dequantize(quantized, block_scale):
    blocks = quantized.reshape(LENGTH, BLOCKS, BLOCK).astype(jnp.float32) * block_scale.T[:, :, None]
    return blocks.reshape(LENGTH, D).astype(jnp.bfloat16)

def clip_logits(quantized, block_scale, slot_params):
    features = dequantize(quantized, block_scale)
    return (features, jnp.dot(features, slot_params, preferred_element_type=jnp.float32))

def reference(tokens, scales, slot_params, expand_weight, expand_bias, reduce_weight, reduce_bias):

    def slot_sums(operands):
        features, logits = clip_logits(operands[0], operands[1], slot_params)
        column_peak = lax.optimization_barrier(jnp.max(logits, axis=0, keepdims=True))
        weights = jnp.exp(logits - column_peak)
        dispatch = (weights / lax.optimization_barrier(jnp.sum(weights, axis=0, keepdims=True))).astype(jnp.bfloat16)
        return jnp.dot(dispatch.T, features, preferred_element_type=jnp.float32).astype(jnp.bfloat16)
    slot_inputs = lax.map(slot_sums, (tokens, scales))
    grouped = slot_inputs.reshape(CLIPS, EXPERTS, SLOTS, D).transpose(1, 0, 2, 3).reshape(EXPERTS, CLIPS * SLOTS, D)

    def expert_apply(operands):
        slot_rows, weight_in, bias_in, weight_out, bias_out = operands
        widened = slot_rows.astype(jnp.float32)
        normalized = (widened * lax.rsqrt(lax.optimization_barrier(jnp.mean(widened * widened, axis=-1, keepdims=True)) + 1e-06)).astype(jnp.bfloat16)
        hidden = jnp.dot(normalized, weight_in, preferred_element_type=jnp.float32) + bias_in.astype(jnp.float32)
        hidden = jax.nn.gelu(hidden, approximate=False).astype(jnp.bfloat16)
        output = jnp.dot(hidden, weight_out, preferred_element_type=jnp.float32) + bias_out.astype(jnp.float32)
        return output.astype(jnp.bfloat16)
    slot_outputs = lax.map(expert_apply, (grouped, expand_weight, expand_bias, reduce_weight, reduce_bias))
    per_clip = slot_outputs.reshape(EXPERTS, CLIPS, SLOTS, D).transpose(1, 0, 2, 3).reshape(CLIPS, SLOTS_ALL, D)

    def combine_clip(operands):
        features, logits = clip_logits(operands[0], operands[1], slot_params)
        row_peak = lax.optimization_barrier(jnp.max(logits, axis=1, keepdims=True))
        weights = jnp.exp(logits - row_peak)
        combine = (weights / lax.optimization_barrier(jnp.sum(weights, axis=1, keepdims=True))).astype(jnp.bfloat16)
        return jnp.dot(combine, operands[2], preferred_element_type=jnp.float32).astype(jnp.bfloat16)
    return lax.map(combine_clip, (tokens, scales, per_clip))
```

```python
import functools
import math

import jax
import jax.numpy as jnp
from jax import lax
from jax.experimental import pallas as pl
from jax.experimental.pallas import tpu as pltpu
from jax.sharding import PartitionSpec as P

F32 = jnp.float32
BF16 = jnp.bfloat16
MESH = pl.DeviceIdType.MESH
CHUNK = 256
HIDDEN_CHUNK = 768


def dot(a, b, contract=((1,), (0,))):
    return lax.dot_general(a, b, (contract, ((), ())), preferred_element_type=F32)


def iota(shape, axis):
    return lax.broadcasted_iota(jnp.int32, shape, axis)


def spread_matrix(groups, rows, piece, parts):
    shape = (groups * rows * parts, groups * rows)
    out, row = iota(shape, 0), iota(shape, 1)
    wide = rows * parts
    target = (row // rows) * wide + piece * rows + row % rows
    return (out == target).astype(F32).astype(BF16)


def gather_matrix(groups, rows, piece, parts):
    shape = (groups * rows, groups * rows * parts)
    row, out = iota(shape, 0), iota(shape, 1)
    wide = rows * parts
    target = (row // rows) * wide + piece * rows + row % rows
    return (out == target).astype(F32).astype(BF16)


def kernel(
    clips,
    shards,
    tokens,
    scales,
    slot_params,
    w1,
    b1,
    w2,
    b2,
    combine,
    returned,
    feat,
    scale_v,
    params_v,
    w1_v,
    b1_v,
    w2_v,
    b2_v,
    logits,
    stats,
    partial,
    sums,
    out_rows,
    in_rows,
    back_out,
    back_in,
    gathered,
    local_sem,
    token_sem,
    send_a,
    recv_a,
    send_b,
    recv_b,
    send_c,
    recv_c,
    send_d,
    recv_d,
    send_e,
    recv_e,
):
    c_me, s_me = lax.axis_index("clip"), lax.axis_index("shard")
    count, dim = feat.shape
    blocks = scale_v.shape[0]
    width = dim // blocks
    slots = params_v.shape[1]
    experts, _, ff = w1_v.shape
    rows = slots // (clips * shards)
    each = rows // experts
    group = clips * rows
    parts = in_rows.shape[1] // rows
    piece_dim = dim // parts
    chunks = count // CHUNK

    def span(i):
        return pl.ds(pl.multiple_of(i * CHUNK, CHUNK), CHUNK)

    load_scale = pltpu.make_async_copy(scales, scale_v, local_sem.at[0])
    load_params = pltpu.make_async_copy(slot_params, params_v, local_sem.at[1])
    load_params.start()
    load_scale.start()
    for i in range(chunks):
        pltpu.make_async_copy(
            tokens.at[pl.ds(i * CHUNK, CHUNK)], feat.at[pl.ds(i * CHUNK, CHUNK)], token_sem.at[i]
        ).start()
    weight_loads = [
        pltpu.make_async_copy(w1, w1_v, local_sem.at[2]),
        pltpu.make_async_copy(b1, b1_v, local_sem.at[3]),
        pltpu.make_async_copy(w2, w2_v, local_sem.at[4]),
        pltpu.make_async_copy(b2, b2_v, local_sem.at[5]),
    ]
    for load in weight_loads:
        load.start()

    barrier = pltpu.get_barrier_semaphore()
    for d in range(1, shards):
        pl.semaphore_signal(
            barrier, inc=1, device_id=(c_me, lax.rem(s_me + d, shards)), device_id_type=MESH
        )
    for d in range(1, clips):
        pl.semaphore_signal(
            barrier, inc=1, device_id=(lax.rem(c_me + d, clips), s_me), device_id_type=MESH
        )

    load_params.wait()
    shape = (slots, slots)
    old, new = iota(shape, 0), iota(shape, 1)
    source = (((new % group) // rows) * shards + new // group) * rows + new % rows
    ordered = dot(params_v[...], (old == source).astype(F32).astype(BF16)).astype(BF16)
    params_v[...] = ordered
    load_scale.wait()

    def logits_step(i, peak):
        at = span(i)
        pltpu.make_async_copy(tokens.at[at], feat.at[at], token_sem.at[i]).wait()
        scale = scale_v[:, at].T
        for b in range(blocks):
            lanes = slice(b * width, (b + 1) * width)
            feat[at, lanes] = (feat[at, lanes].astype(F32) * scale[:, b : b + 1]).astype(BF16)
        value = dot(feat[at, :], params_v[...])
        logits[at, :] = value
        return jnp.maximum(peak, jnp.max(value, axis=0, keepdims=True))

    peak = lax.fori_loop(0, chunks, logits_step, jnp.full((1, slots), -jnp.inf, F32))

    def sum_step(i, total):
        return total + jnp.sum(jnp.exp(logits[span(i), :] - peak), axis=0, keepdims=True)

    total = lax.fori_loop(0, chunks, sum_step, jnp.zeros((1, slots), F32))
    which = iota((8, slots), 0)
    stats[s_me] = jnp.where(which == 0, peak, total)

    pl.semaphore_wait(barrier, shards - 1 + clips - 1)

    def shard_copies(make):
        return [make(d, lax.rem(s_me + d, shards)) for d in range(1, shards)]

    def clip_copies(make):
        return [make(d, lax.rem(c_me + d, clips)) for d in range(1, clips)]

    stats_sent = shard_copies(
        lambda d, to: pltpu.make_async_remote_copy(
            src_ref=stats.at[s_me],
            dst_ref=stats.at[s_me],
            send_sem=send_a.at[d],
            recv_sem=recv_a.at[s_me],
            device_id=(c_me, to),
            device_id_type=MESH,
        )
    )
    for copy in stats_sent:
        copy.start()

    def combine_step(i, carry):
        at = span(i)
        value = logits[at, :]
        weights = jnp.exp(value - jnp.max(value, axis=1, keepdims=True))
        combine[at, :] = (weights / jnp.sum(weights, axis=1, keepdims=True)).astype(BF16)
        return carry

    lax.fori_loop(0, chunks, combine_step, 0)

    def arrivals(me, size, ref, recv):
        for d in range(1, size):
            origin = lax.rem(me + d, size)
            pltpu.make_async_copy(ref.at[origin], ref.at[origin], recv.at[origin]).wait()

    arrivals(s_me, shards, stats, recv_a)
    top = stats[0, 0:1, :]
    for s in range(1, shards):
        top = jnp.maximum(top, stats[s, 0:1, :])
    total = jnp.zeros((1, slots), F32)
    for s in range(shards):
        total = total + stats[s, 1:2, :] * jnp.exp(stats[s, 0:1, :] - top)

    partial[...] = jnp.zeros(partial.shape, F32)

    def partial_step(i, carry):
        at = span(i)
        dispatch = (jnp.exp(logits[at, :] - top) / total).astype(BF16)
        part = dot(dispatch, feat[at, :], ((0,), (0,)))
        partial[...] += part.reshape(partial.shape)
        return carry

    lax.fori_loop(0, chunks, partial_step, 0)

    sums_sent = shard_copies(
        lambda d, to: pltpu.make_async_remote_copy(
            src_ref=partial.at[to],
            dst_ref=sums.at[s_me],
            send_sem=send_b.at[d],
            recv_sem=recv_b.at[s_me],
            device_id=(c_me, to),
            device_id_type=MESH,
        )
    )
    for copy in sums_sent:
        copy.start()
    sums[s_me] = partial[s_me]
    arrivals(s_me, shards, sums, recv_b)
    value = sums[0]
    for s in range(1, shards):
        value = value + sums[s]
    value = value.astype(BF16)

    def spread(value):
        spreads = [
            dot(
                spread_matrix(clips, rows, p, parts),
                value[:, p * piece_dim : (p + 1) * piece_dim],
            )
            for p in range(parts)
        ]
        return sum(spreads[1:], spreads[0]).reshape(clips, rows * parts, piece_dim)

    def unspread(value):
        value = value.reshape(clips * rows * parts, piece_dim).astype(BF16)
        return jnp.concatenate(
            [dot(gather_matrix(clips, rows, p, parts), value) for p in range(parts)], axis=1
        )

    def exchange(source, target, send, recv):
        target[c_me] = source[c_me]
        sent = clip_copies(
            lambda d, to: pltpu.make_async_remote_copy(
                src_ref=source.at[to],
                dst_ref=target.at[c_me],
                send_sem=send.at[d],
                recv_sem=recv.at[c_me],
                device_id=(to, s_me),
                device_id_type=MESH,
            )
        )
        for copy in sent:
            copy.start()
        arrivals(c_me, clips, target, recv)
        return sent

    out_rows[...] = spread(value)
    rows_sent = exchange(out_rows, in_rows, send_c, recv_c)

    wide = unspread(in_rows[...])
    mean = jnp.mean(wide * wide, axis=-1, keepdims=True)
    normalized = (wide * lax.rsqrt(mean + 1e-06)).astype(BF16)
    for load in weight_loads:
        load.wait()

    def mine(shape, expert):
        return (iota(shape, 0) % rows) // each == expert

    def choose(values):
        chosen = values[0]
        for e in range(1, experts):
            chosen = jnp.where(mine(chosen.shape, e), values[e], chosen)
        return chosen

    def spread_bias(ref, at):
        value = ref[:, at].astype(F32)
        size = (group, value.shape[1])
        return choose([jnp.broadcast_to(value[e : e + 1], size) for e in range(experts)])

    def expert_step(f, outs):
        at = pl.ds(pl.multiple_of(f * HIDDEN_CHUNK, HIDDEN_CHUNK), HIDDEN_CHUNK)
        before = choose([dot(normalized, w1_v[e, :, at]) for e in range(experts)])
        before = before + spread_bias(b1_v, at)
        hidden = (0.5 * before * (1.0 + lax.erf(before * math.sqrt(0.5)))).astype(BF16)
        return tuple(outs[e] + dot(hidden, w2_v[e, at, :]) for e in range(experts))

    outs = tuple(jnp.zeros((group, dim), F32) for _ in range(experts))
    outs = lax.fori_loop(0, ff // HIDDEN_CHUNK, expert_step, outs)
    result = (choose(outs) + spread_bias(b2_v, slice(None))).astype(BF16)

    back_out[...] = spread(result)
    back_sent = exchange(back_out, back_in, send_d, recv_d)
    gathered[s_me] = unspread(back_in[...]).astype(BF16)
    last_sent = shard_copies(
        lambda d, to: pltpu.make_async_remote_copy(
            src_ref=gathered.at[s_me],
            dst_ref=gathered.at[s_me],
            send_sem=send_e.at[d],
            recv_sem=recv_e.at[s_me],
            device_id=(c_me, to),
            device_id_type=MESH,
        )
    )
    for copy in last_sent:
        copy.start()
    arrivals(s_me, shards, gathered, recv_e)
    returned[...] = gathered[...].reshape(returned.shape)
    for copy in stats_sent + sums_sent + rows_sent + back_sent + last_sent:
        copy.wait_send()


def local(clips, shards, tokens, scales, slot_params, w1, b1, w2, b2):
    count, dim = tokens.shape[1:]
    blocks = scales.shape[1]
    slots = slot_params.shape[1]
    rows = slots // (clips * shards)
    group = clips * rows
    parts = 8 // rows
    piece = (clips, rows * parts, dim // parts)
    combine, returned = pl.pallas_call(
        functools.partial(kernel, clips, shards),
        out_shape=(
            jax.ShapeDtypeStruct((count, slots), BF16),
            jax.ShapeDtypeStruct((slots, dim), BF16),
        ),
        in_specs=[pl.BlockSpec(memory_space=pl.ANY)] * 7,
        out_specs=(pl.BlockSpec(memory_space=pltpu.VMEM),) * 2,
        scratch_shapes=[
            pltpu.VMEM((count, dim), BF16),
            pltpu.VMEM((blocks, count), F32),
            pltpu.VMEM(slot_params.shape, BF16),
            pltpu.VMEM(w1.shape, BF16),
            pltpu.VMEM(b1.shape, BF16),
            pltpu.VMEM(w2.shape, BF16),
            pltpu.VMEM(b2.shape, BF16),
            pltpu.VMEM((count, slots), F32),
            pltpu.VMEM((shards, 8, slots), F32),
            pltpu.VMEM((shards, group, dim), F32),
            pltpu.VMEM((shards, group, dim), F32),
            pltpu.VMEM(piece, F32),
            pltpu.VMEM(piece, F32),
            pltpu.VMEM(piece, F32),
            pltpu.VMEM(piece, F32),
            pltpu.VMEM((shards, group, dim), BF16),
            pltpu.SemaphoreType.DMA((6,)),
            pltpu.SemaphoreType.DMA((count // CHUNK,)),
            pltpu.SemaphoreType.DMA((shards,)),
            pltpu.SemaphoreType.DMA((shards,)),
            pltpu.SemaphoreType.DMA((shards,)),
            pltpu.SemaphoreType.DMA((shards,)),
            pltpu.SemaphoreType.DMA((clips,)),
            pltpu.SemaphoreType.DMA((clips,)),
            pltpu.SemaphoreType.DMA((clips,)),
            pltpu.SemaphoreType.DMA((clips,)),
            pltpu.SemaphoreType.DMA((shards,)),
            pltpu.SemaphoreType.DMA((shards,)),
        ],
        compiler_params=pltpu.CompilerParams(
            collective_id=0, has_side_effects=True, vmem_limit_bytes=56 << 20
        ),
        name="slots",
    )(tokens[0], scales[0], slot_params, w1, b1, w2, b2)
    mixed = jnp.dot(combine, returned, preferred_element_type=F32).astype(BF16)
    return mixed[None]


def solution(mesh):
    placed = (
        P("clip", "shard", None),
        P("clip", None, "shard"),
        P(),
        P(("clip", "shard"), None, None),
        P(("clip", "shard"), None),
        P(("clip", "shard"), None, None),
        P(("clip", "shard"), None),
    )
    return jax.shard_map(
        functools.partial(local, mesh.shape["clip"], mesh.shape["shard"]),
        mesh=mesh,
        in_specs=placed,
        out_specs=P("clip", "shard", None),
        check_vma=False,
    )
```

```python
import functools
import math

import jax
import jax.numpy as jnp
from jax import lax
from jax.experimental import pallas as pl
from jax.experimental.pallas import tpu as pltpu
from jax.sharding import PartitionSpec as P

F32 = jnp.float32
BF16 = jnp.bfloat16
MESH = pl.DeviceIdType.MESH
CHUNK = 256
HIDDEN_CHUNK = 768
MIX_ROWS = 384


def dot(a, b, contract=((1,), (0,))):
    return lax.dot_general(a, b, (contract, ((), ())), preferred_element_type=F32)


def iota(shape, axis):
    return lax.broadcasted_iota(jnp.int32, shape, axis)


def top_half(shape, rows):
    return iota(shape, 0) % (2 * rows) < rows


def spread(value, rows):
    count, dim = value.shape
    left, right = value[:, : dim // 2], value[:, dim // 2 :]
    top = top_half(left.shape, rows)
    even = jnp.where(top, left, pltpu.roll(right, rows, 0))
    odd = jnp.where(top, pltpu.roll(left, count - rows, 0), right)
    shape = (count // (2 * rows), 2 * rows, dim // 2)
    return even.reshape(shape), odd.reshape(shape)


def unspread(even, odd, rows):
    shape = (even.shape[0] * 2 * rows, even.shape[2])
    even, odd = even.reshape(shape), odd.reshape(shape)
    top = top_half(shape, rows)
    left = jnp.where(top, even, pltpu.roll(odd, rows, 0))
    right = jnp.where(top, pltpu.roll(even, shape[0] - rows, 0), odd)
    return jnp.concatenate([left, right], axis=1)


def kernel(
    clips,
    shards,
    tokens,
    scales,
    slot_params,
    w1,
    b1,
    w2,
    b2,
    combine,
    returned,
    feat,
    scale_v,
    params_v,
    w1_v,
    b1_v,
    w2_v,
    b2_v,
    logits,
    lifted,
    combine_v,
    stats,
    partial,
    partial_out,
    sums,
    back_out,
    back_in,
    local_sem,
    token_sem,
    send_a,
    recv_a,
    send_b,
    recv_b,
    send_c,
    recv_c,
):
    c_me, s_me = lax.axis_index("clip"), lax.axis_index("shard")
    count, dim = feat.shape
    blocks = scale_v.shape[0]
    width = dim // blocks
    slots = params_v.shape[1]
    experts, _, ff = w1_v.shape
    rows = slots // (clips * shards)
    each = rows // experts
    group = clips * rows
    devices = clips * shards
    me = c_me * shards + s_me
    chunks = count // CHUNK

    def span(i):
        return pl.ds(pl.multiple_of(i * CHUNK, CHUNK), CHUNK)

    load_scale = pltpu.make_async_copy(scales, scale_v, local_sem.at[0])
    load_params = pltpu.make_async_copy(slot_params, params_v, local_sem.at[1])
    load_params.start()
    load_scale.start()
    for i in range(chunks):
        pltpu.make_async_copy(
            tokens.at[pl.ds(i * CHUNK, CHUNK)], feat.at[pl.ds(i * CHUNK, CHUNK)], token_sem.at[i]
        ).start()
    weight_loads = [
        pltpu.make_async_copy(w1, w1_v, local_sem.at[2]),
        pltpu.make_async_copy(b1, b1_v, local_sem.at[3]),
        pltpu.make_async_copy(w2, w2_v, local_sem.at[4]),
        pltpu.make_async_copy(b2, b2_v, local_sem.at[5]),
    ]
    for load in weight_loads:
        load.start()

    barrier = pltpu.get_barrier_semaphore()

    def place(d):
        at = lax.rem(me + d, devices)
        return at, at // shards, lax.rem(at, shards)

    def greet(d, carry):
        _, c, s = place(d)
        pl.semaphore_signal(barrier, inc=1, device_id=(c, s), device_id_type=MESH)
        return carry

    lax.fori_loop(1, devices, greet, 0)
    load_params.wait()
    load_scale.wait()

    def logits_step(i, peak):
        at = span(i)
        pltpu.make_async_copy(tokens.at[at], feat.at[at], token_sem.at[i]).wait()
        scale = scale_v[:, 0, at].T
        for b in range(blocks):
            lanes = slice(b * width, (b + 1) * width)
            feat[at, lanes] = (feat[at, lanes].astype(F32) * scale[:, b : b + 1]).astype(BF16)
        value = dot(feat[at, :], params_v[...])
        logits[at, :] = value
        return jnp.maximum(peak, jnp.max(value, axis=0, keepdims=True))

    peak = lax.fori_loop(0, chunks, logits_step, jnp.full((1, slots), -jnp.inf, F32))

    def sum_step(i, total):
        at = span(i)
        value = jnp.exp(logits[at, :] - peak)
        lifted[at, :] = value
        return total + jnp.sum(value, axis=0, keepdims=True)

    total = lax.fori_loop(0, chunks, sum_step, jnp.zeros((1, slots), F32))
    which = iota((8, slots), 0)
    stats[s_me] = jnp.where(which == 0, peak, total)

    pl.semaphore_wait(barrier, devices - 1)

    def shard_copies(make):
        return [make(d, lax.rem(s_me + d, shards)) for d in range(1, shards)]

    stats_sent = shard_copies(
        lambda d, to: pltpu.make_async_remote_copy(
            src_ref=stats.at[s_me],
            dst_ref=stats.at[s_me],
            send_sem=send_a.at[d],
            recv_sem=recv_a.at[s_me],
            device_id=(c_me, to),
            device_id_type=MESH,
        )
    )
    for copy in stats_sent:
        copy.start()

    for d in range(1, shards):
        origin = lax.rem(s_me + d, shards)
        pltpu.make_async_copy(stats.at[origin], stats.at[origin], recv_a.at[origin]).wait()
    top = stats[0, 0:1, :]
    for s in range(1, shards):
        top = jnp.maximum(top, stats[s, 0:1, :])
    total = jnp.zeros((1, slots), F32)
    for s in range(shards):
        total = total + stats[s, 1:2, :] * jnp.exp(stats[s, 0:1, :] - top)

    lift = jnp.exp(peak - top) / total
    partial[...] = jnp.zeros(partial.shape, F32)

    def partial_step(i, carry):
        at = span(i)
        dispatch = (lifted[at, :] * lift).astype(BF16)
        partial[...] += dot(dispatch, feat[at, :], ((0,), (0,)))
        return carry

    lax.fori_loop(0, chunks, partial_step, 0)
    even, odd = spread(partial[...], rows)
    partial_out[:, 0] = even
    partial_out[:, 1] = odd

    def send_sum(d):
        to, c, s = place(d)
        return pltpu.make_async_remote_copy(
            src_ref=partial_out.at[to // 2, lax.rem(to, 2)],
            dst_ref=sums.at[s_me, c_me // 2, lax.rem(c_me, 2)],
            send_sem=send_b.at[d],
            recv_sem=recv_b.at[me],
            device_id=(c, s),
            device_id_type=MESH,
        )

    def start_sum(d, carry):
        send_sum(d).start()
        return carry

    lax.fori_loop(1, devices, start_sum, 0)
    sums[s_me, c_me // 2, lax.rem(c_me, 2)] = partial_out[me // 2, lax.rem(me, 2)]

    def combine_step(i, carry):
        at = span(i)
        value = logits[at, :]
        weights = jnp.exp(value - jnp.max(value, axis=1, keepdims=True))
        combine_v[at, :] = (weights / jnp.sum(weights, axis=1, keepdims=True)).astype(BF16)
        return carry

    lax.fori_loop(0, chunks, combine_step, 0)
    store = pltpu.make_async_copy(combine_v, combine, local_sem.at[6])
    store.start()

    def await_sum(d, carry):
        origin, c, s = place(d)
        landed = sums.at[s, c // 2, lax.rem(c, 2)]
        pltpu.make_async_copy(landed, landed, recv_b.at[origin]).wait()
        return carry

    lax.fori_loop(1, devices, await_sum, 0)
    value = sums[0]
    for s in range(1, shards):
        value = value + sums[s]
    wide = unspread(value[:, 0], value[:, 1], rows).astype(BF16).astype(F32)

    mean = jnp.mean(wide * wide, axis=-1, keepdims=True)
    normalized = (wide * lax.rsqrt(mean + 1e-06)).astype(BF16)
    for load in weight_loads:
        load.wait()

    def mine(shape, expert):
        return (iota(shape, 0) % rows) // each == expert

    def choose(values):
        chosen = values[0]
        for e in range(1, experts):
            chosen = jnp.where(mine(chosen.shape, e), values[e], chosen)
        return chosen

    def spread_bias(ref, at):
        value = ref[:, at].astype(F32)
        size = (group, value.shape[1])
        return choose([jnp.broadcast_to(value[e : e + 1], size) for e in range(experts)])

    def expert_step(f, outs):
        at = pl.ds(pl.multiple_of(f * HIDDEN_CHUNK, HIDDEN_CHUNK), HIDDEN_CHUNK)
        before = choose([dot(normalized, w1_v[e, :, at]) for e in range(experts)])
        before = before + spread_bias(b1_v, at)
        hidden = (0.5 * before * (1.0 + lax.erf(before * math.sqrt(0.5)))).astype(BF16)
        return tuple(outs[e] + dot(hidden, w2_v[e, at, :]) for e in range(experts))

    outs = tuple(jnp.zeros((group, dim), F32) for _ in range(experts))
    outs = lax.fori_loop(0, ff // HIDDEN_CHUNK, expert_step, outs, unroll=True)
    result = (choose(outs) + spread_bias(b2_v, slice(None))).astype(BF16).astype(F32)
    even, odd = spread(result, rows)
    back_out[:, 0] = even.astype(BF16)
    back_out[:, 1] = odd.astype(BF16)

    def send_back(d):
        to, c, s = place(d)
        return pltpu.make_async_remote_copy(
            src_ref=back_out.at[c // 2, lax.rem(c, 2)],
            dst_ref=back_in.at[me // 2, lax.rem(me, 2)],
            send_sem=send_c.at[d],
            recv_sem=recv_c.at[me],
            device_id=(c, s),
            device_id_type=MESH,
        )

    def start_back(d, carry):
        send_back(d).start()
        return carry

    lax.fori_loop(1, devices, start_back, 0)
    back_in[me // 2, lax.rem(me, 2)] = back_out[c_me // 2, lax.rem(c_me, 2)]
    for copy in stats_sent:
        copy.wait_send()
    store.wait()

    def await_back(d, carry):
        origin, c, s = place(d)
        landed = back_in.at[origin // 2, lax.rem(origin, 2)]
        pltpu.make_async_copy(landed, landed, recv_c.at[origin]).wait()
        return carry

    lax.fori_loop(1, devices, await_back, 0)
    value = back_in[...].astype(F32)
    returned[...] = unspread(value[:, 0], value[:, 1], rows).astype(BF16)

    def finish(d, carry):
        send_sum(d).wait_send()
        send_back(d).wait_send()
        return carry

    lax.fori_loop(1, devices, finish, 0)


def mix(combine, returned, mixed):
    mixed[...] = dot(combine[...], returned[...]).astype(BF16)


def local(clips, shards, tokens, scales, slot_params, w1, b1, w2, b2):
    count, dim = tokens.shape[1:]
    blocks = scales.shape[1]
    slots = slot_params.shape[1]
    rows = slots // (clips * shards)
    devices = clips * shards
    piece = (2, 2 * rows, dim // 2)
    combine, returned = pl.pallas_call(
        functools.partial(kernel, clips, shards),
        out_shape=(
            jax.ShapeDtypeStruct((count, slots), BF16),
            jax.ShapeDtypeStruct((slots, dim), BF16),
        ),
        in_specs=[pl.BlockSpec(memory_space=pl.ANY)] * 7,
        out_specs=(pl.BlockSpec(memory_space=pl.ANY), pl.BlockSpec(memory_space=pltpu.VMEM)),
        scratch_shapes=[
            pltpu.VMEM((count, dim), BF16),
            pltpu.VMEM((blocks, 1, count), F32),
            pltpu.VMEM(slot_params.shape, BF16),
            pltpu.VMEM(w1.shape, BF16),
            pltpu.VMEM(b1.shape, BF16),
            pltpu.VMEM(w2.shape, BF16),
            pltpu.VMEM(b2.shape, BF16),
            pltpu.VMEM((count, slots), F32),
            pltpu.VMEM((count, slots), F32),
            pltpu.VMEM((count, slots), BF16),
            pltpu.VMEM((shards, 8, slots), F32),
            pltpu.VMEM((slots, dim), F32),
            pltpu.VMEM((devices // 2,) + piece, F32),
            pltpu.VMEM((shards, clips // 2) + piece, F32),
            pltpu.VMEM((clips // 2,) + piece, BF16),
            pltpu.VMEM((devices // 2,) + piece, BF16),
            pltpu.SemaphoreType.DMA((7,)),
            pltpu.SemaphoreType.DMA((count // CHUNK,)),
            pltpu.SemaphoreType.DMA((shards,)),
            pltpu.SemaphoreType.DMA((shards,)),
            pltpu.SemaphoreType.DMA((devices,)),
            pltpu.SemaphoreType.DMA((devices,)),
            pltpu.SemaphoreType.DMA((devices,)),
            pltpu.SemaphoreType.DMA((devices,)),
        ],
        compiler_params=pltpu.CompilerParams(
            collective_id=0, has_side_effects=True, vmem_limit_bytes=56 << 20
        ),
        name="slots",
    )(tokens[0], scales.transpose(1, 0, 2), slot_params, w1, b1, w2, b2)
    mixed = pl.pallas_call(
        mix,
        grid=(count // MIX_ROWS,),
        out_shape=jax.ShapeDtypeStruct((count, dim), BF16),
        in_specs=[
            pl.BlockSpec((MIX_ROWS, slots), lambda i: (i, 0)),
            pl.BlockSpec((slots, dim), lambda i: (0, 0)),
        ],
        out_specs=pl.BlockSpec((MIX_ROWS, dim), lambda i: (i, 0)),
        name="mix",
    )(combine, returned)
    return mixed[None]


def solution(mesh):
    placed = (
        P("clip", "shard", None),
        P("clip", None, "shard"),
        P(),
        P(("clip", "shard"), None, None),
        P(("clip", "shard"), None),
        P(("clip", "shard"), None, None),
        P(("clip", "shard"), None),
    )
    return jax.shard_map(
        functools.partial(local, mesh.shape["clip"], mesh.shape["shard"]),
        mesh=mesh,
        in_specs=placed,
        out_specs=P("clip", "shard", None),
        check_vma=False,
    )
```

```python
import functools
import math

import jax
import jax.numpy as jnp
from jax import lax
from jax.experimental import pallas as pl
from jax.experimental.pallas import tpu as pltpu
from jax.sharding import PartitionSpec as P

F32 = jnp.float32
BF16 = jnp.bfloat16
MESH = pl.DeviceIdType.MESH
CHUNK = 256
HIDDEN_CHUNK = 768


def dot(a, b, contract=((1,), (0,))):
    return lax.dot_general(a, b, (contract, ((), ())), preferred_element_type=F32)


def iota(shape, axis):
    return lax.broadcasted_iota(jnp.int32, shape, axis)


def top_half(shape, rows):
    return iota(shape, 0) % (2 * rows) < rows


def spread(value, rows):
    count, dim = value.shape
    left, right = value[:, : dim // 2], value[:, dim // 2 :]
    top = top_half(left.shape, rows)
    even = jnp.where(top, left, pltpu.roll(right, rows, 0))
    odd = jnp.where(top, pltpu.roll(left, count - rows, 0), right)
    shape = (count // (2 * rows), 2 * rows, dim // 2)
    return even.reshape(shape), odd.reshape(shape)


def unspread(even, odd, rows):
    shape = (even.shape[0] * 2 * rows, even.shape[2])
    even, odd = even.reshape(shape), odd.reshape(shape)
    top = top_half(shape, rows)
    left = jnp.where(top, even, pltpu.roll(odd, rows, 0))
    right = jnp.where(top, pltpu.roll(even, shape[0] - rows, 0), odd)
    return jnp.concatenate([left, right], axis=1)


def kernel(
    clips,
    shards,
    tokens,
    scales,
    slot_params,
    w1,
    b1,
    w2,
    b2,
    combine,
    returned,
    feat,
    scale_v,
    params_v,
    w1_v,
    b1_v,
    w2_v,
    b2_v,
    logits,
    lifted,
    combine_v,
    stats_out,
    stats,
    partial_out,
    sums,
    back_out,
    back_in,
    local_sem,
    token_sem,
    send_a,
    recv_a,
    send_b,
    recv_b,
    send_c,
    recv_c,
):
    c_me, s_me = lax.axis_index("clip"), lax.axis_index("shard")
    count, dim = feat.shape
    blocks = scale_v.shape[0]
    width = dim // blocks
    slots = params_v.shape[1]
    experts, _, ff = w1_v.shape
    rows = slots // (clips * shards)
    each = rows // experts
    group = clips * rows
    devices = clips * shards
    me = c_me * shards + s_me
    chunks = count // CHUNK

    def span(i):
        return pl.ds(i * CHUNK, CHUNK)

    load_scale = pltpu.make_async_copy(scales, scale_v, local_sem.at[0])
    load_params = pltpu.make_async_copy(slot_params, params_v, local_sem.at[1])
    load_params.start()
    load_scale.start()
    for i in range(chunks):
        pltpu.make_async_copy(
            tokens.at[pl.ds(i * CHUNK, CHUNK)], feat.at[pl.ds(i * CHUNK, CHUNK)], token_sem.at[i]
        ).start()
    weight_loads = [
        pltpu.make_async_copy(w1, w1_v, local_sem.at[2]),
        pltpu.make_async_copy(b1, b1_v, local_sem.at[3]),
        pltpu.make_async_copy(w2, w2_v, local_sem.at[4]),
        pltpu.make_async_copy(b2, b2_v, local_sem.at[5]),
    ]
    for load in weight_loads:
        load.start()

    barrier = pltpu.get_barrier_semaphore()

    def place(d):
        at = lax.rem(me + d, devices)
        return at, at // shards, lax.rem(at, shards)

    def greet(d, carry):
        _, c, s = place(d)
        pl.semaphore_signal(barrier, inc=1, device_id=(c, s), device_id_type=MESH)
        return carry

    lax.fori_loop(1, devices, greet, 0)
    load_params.wait()
    load_scale.wait()

    peak = jnp.full((1, slots), -jnp.inf, F32)
    for i in range(chunks):
        at = span(i)
        pltpu.make_async_copy(tokens.at[at], feat.at[at], token_sem.at[i]).wait()
        scale = scale_v[:, 0, at].T
        scaled = jnp.concatenate(
            [
                feat[at, b * width : (b + 1) * width].astype(F32) * scale[:, b : b + 1]
                for b in range(blocks)
            ],
            axis=1,
        ).astype(BF16)
        feat[at, :] = scaled
        value = dot(scaled, params_v[...])
        logits[at, :] = value
        peak = jnp.maximum(peak, jnp.max(value, axis=0, keepdims=True))

    total = jnp.zeros((1, slots), F32)
    for i in range(chunks):
        at = span(i)
        value = jnp.exp(logits[at, :] - peak)
        total = total + jnp.sum(value, axis=0, keepdims=True)
        high = value.astype(BF16)
        low = (value - high.astype(F32)).astype(BF16)
        lifted[at, :slots] = high
        lifted[at, slots:] = low
    stats_out[0:1, :] = peak
    stats_out[1:2, :] = total
    stats[me] = stats_out[...]
    partial = dot(lifted[...], feat[...], ((0,), (0,)))
    partial = partial[:slots] + partial[slots:]
    even, odd = spread(partial, rows)
    partial_out[:, 0] = even
    partial_out[:, 1] = odd

    pl.semaphore_wait(barrier, devices - 1)

    def send_stats(d):
        _, c, s = place(d)
        return pltpu.make_async_remote_copy(
            src_ref=stats_out,
            dst_ref=stats.at[me],
            send_sem=send_a.at[d],
            recv_sem=recv_a.at[me],
            device_id=(c, s),
            device_id_type=MESH,
        )

    def send_sum(d):
        to, c, s = place(d)
        return pltpu.make_async_remote_copy(
            src_ref=partial_out.at[to // 2, lax.rem(to, 2)],
            dst_ref=sums.at[s_me, c_me // 2, lax.rem(c_me, 2)],
            send_sem=send_b.at[d],
            recv_sem=recv_b.at[me],
            device_id=(c, s),
            device_id_type=MESH,
        )

    def start_sum(d, carry):
        send_sum(d).start()
        send_stats(d).start()
        return carry

    lax.fori_loop(1, devices, start_sum, 0)
    sums[s_me, c_me // 2, lax.rem(c_me, 2)] = partial_out[me // 2, lax.rem(me, 2)]

    for i in range(chunks):
        at = span(i)
        value = logits[at, :]
        weights = jnp.exp(value - jnp.max(value, axis=1, keepdims=True))
        combine_v[at, :] = (weights / jnp.sum(weights, axis=1, keepdims=True)).astype(BF16)
    store = pltpu.make_async_copy(combine_v, combine, local_sem.at[6])
    store.start()

    def await_sum(d, carry):
        origin, c, s = place(d)
        landed = sums.at[s, c // 2, lax.rem(c, 2)]
        pltpu.make_async_copy(landed, landed, recv_b.at[origin]).wait()
        pltpu.make_async_copy(stats.at[origin], stats.at[origin], recv_a.at[origin]).wait()
        return carry

    lax.fori_loop(1, devices, await_sum, 0)
    lane = iota((2 * rows, slots), 1) == me * rows + iota((2 * rows, slots), 0) % rows
    share = stats[...].reshape(clips, shards, 2, slots)
    weighted = []
    for c in range(clips):
        peaks = [share[c, s, 0:1] for s in range(shards)]
        top = functools.reduce(jnp.maximum, peaks)
        lifts = [jnp.exp(peaks[s] - top) for s in range(shards)]
        total = sum(share[c, s, 1:2] * lifts[s] for s in range(shards))
        value = jnp.zeros(sums.shape[3:], F32)
        for s in range(shards):
            own = jnp.sum(jnp.where(lane, lifts[s] / total, 0.0), axis=1, keepdims=True)
            value = value + sums[s, c // 2, c % 2] * own
        weighted.append(value[None])
    even, odd = (jnp.concatenate(weighted[p::2], axis=0) for p in range(2))
    wide = unspread(even, odd, rows).astype(BF16).astype(F32)

    mean = jnp.mean(wide * wide, axis=-1, keepdims=True)
    normalized = (wide * lax.rsqrt(mean + 1e-06)).astype(BF16)
    for load in weight_loads:
        load.wait()

    def mine(shape, expert):
        return (iota(shape, 0) % rows) // each == expert

    def choose(values):
        chosen = values[0]
        for e in range(1, experts):
            chosen = jnp.where(mine(chosen.shape, e), values[e], chosen)
        return chosen

    def spread_bias(ref, at):
        value = ref[:, at].astype(F32)
        size = (group, value.shape[1])
        return choose([jnp.broadcast_to(value[e : e + 1], size) for e in range(experts)])

    def expert_step(f, outs):
        at = pl.ds(pl.multiple_of(f * HIDDEN_CHUNK, HIDDEN_CHUNK), HIDDEN_CHUNK)
        before = choose([dot(normalized, w1_v[e, :, at]) for e in range(experts)])
        before = before + spread_bias(b1_v, at)
        hidden = (0.5 * before * (1.0 + lax.erf(before * math.sqrt(0.5)))).astype(BF16)
        return tuple(outs[e] + dot(hidden, w2_v[e, at, :]) for e in range(experts))

    outs = tuple(jnp.zeros((group, dim), F32) for _ in range(experts))
    outs = lax.fori_loop(0, ff // HIDDEN_CHUNK, expert_step, outs, unroll=True)
    result = (choose(outs) + spread_bias(b2_v, slice(None))).astype(BF16).astype(F32)
    even, odd = spread(result, rows)
    back_out[:, 0] = even.astype(BF16)
    back_out[:, 1] = odd.astype(BF16)

    def send_back(d):
        to, c, s = place(d)
        return pltpu.make_async_remote_copy(
            src_ref=back_out.at[c // 2, lax.rem(c, 2)],
            dst_ref=back_in.at[me // 2, lax.rem(me, 2)],
            send_sem=send_c.at[d],
            recv_sem=recv_c.at[me],
            device_id=(c, s),
            device_id_type=MESH,
        )

    def start_back(d, carry):
        send_back(d).start()
        return carry

    lax.fori_loop(1, devices, start_back, 0)
    back_in[me // 2, lax.rem(me, 2)] = back_out[c_me // 2, lax.rem(c_me, 2)]
    store.wait()

    def await_back(d, carry):
        origin, c, s = place(d)
        landed = back_in.at[origin // 2, lax.rem(origin, 2)]
        pltpu.make_async_copy(landed, landed, recv_c.at[origin]).wait()
        return carry

    lax.fori_loop(1, devices, await_back, 0)
    value = back_in[...].astype(F32)
    returned[...] = unspread(value[:, 0], value[:, 1], rows).astype(BF16)

    def finish(d, carry):
        send_stats(d).wait_send()
        send_sum(d).wait_send()
        send_back(d).wait_send()
        return carry

    lax.fori_loop(1, devices, finish, 0)


def local(clips, shards, tokens, scales, slot_params, w1, b1, w2, b2):
    count, dim = tokens.shape[1:]
    blocks = scales.shape[1]
    slots = slot_params.shape[1]
    rows = slots // (clips * shards)
    devices = clips * shards
    piece = (2, 2 * rows, dim // 2)
    combine, returned = pl.pallas_call(
        functools.partial(kernel, clips, shards),
        out_shape=(
            jax.ShapeDtypeStruct((count, slots), BF16),
            jax.ShapeDtypeStruct((slots, dim), BF16),
        ),
        in_specs=[pl.BlockSpec(memory_space=pl.ANY)] * 7,
        out_specs=(pl.BlockSpec(memory_space=pl.ANY), pl.BlockSpec(memory_space=pltpu.VMEM)),
        scratch_shapes=[
            pltpu.VMEM((count, dim), BF16),
            pltpu.VMEM((blocks, 1, count), F32),
            pltpu.VMEM(slot_params.shape, BF16),
            pltpu.VMEM(w1.shape, BF16),
            pltpu.VMEM(b1.shape, BF16),
            pltpu.VMEM(w2.shape, BF16),
            pltpu.VMEM(b2.shape, BF16),
            pltpu.VMEM((count, slots), F32),
            pltpu.VMEM((count, 2 * slots), BF16),
            pltpu.VMEM((count, slots), BF16),
            pltpu.VMEM((2, slots), F32),
            pltpu.VMEM((devices, 2, slots), F32),
            pltpu.VMEM((devices // 2,) + piece, F32),
            pltpu.VMEM((shards, clips // 2) + piece, F32),
            pltpu.VMEM((clips // 2,) + piece, BF16),
            pltpu.VMEM((devices // 2,) + piece, BF16),
            pltpu.SemaphoreType.DMA((7,)),
            pltpu.SemaphoreType.DMA((count // CHUNK,)),
            pltpu.SemaphoreType.DMA((devices,)),
            pltpu.SemaphoreType.DMA((devices,)),
            pltpu.SemaphoreType.DMA((devices,)),
            pltpu.SemaphoreType.DMA((devices,)),
            pltpu.SemaphoreType.DMA((devices,)),
            pltpu.SemaphoreType.DMA((devices,)),
        ],
        compiler_params=pltpu.CompilerParams(
            collective_id=0, has_side_effects=True, vmem_limit_bytes=56 << 20
        ),
        name="slots",
    )(tokens[0], scales.transpose(1, 0, 2), slot_params, w1, b1, w2, b2)
    mixed = jnp.dot(combine, returned, preferred_element_type=F32).astype(BF16)
    return mixed[None]


def solution(mesh):
    placed = (
        P("clip", "shard", None),
        P("clip", None, "shard"),
        P(),
        P(("clip", "shard"), None, None),
        P(("clip", "shard"), None),
        P(("clip", "shard"), None, None),
        P(("clip", "shard"), None),
    )
    return jax.shard_map(
        functools.partial(local, mesh.shape["clip"], mesh.shape["shard"]),
        mesh=mesh,
        in_specs=placed,
        out_specs=P("clip", "shard", None),
        check_vma=False,
    )
```

```python
import functools
import math

import jax
import jax.numpy as jnp
from jax import lax
from jax.experimental import pallas as pl
from jax.experimental.pallas import tpu as pltpu
from jax.sharding import PartitionSpec as P

F32 = jnp.float32
BF16 = jnp.bfloat16
MESH = pl.DeviceIdType.MESH
CHUNK = 256
HIDDEN_CHUNK = 768


def dot(a, b, contract=((1,), (0,))):
    return lax.dot_general(a, b, (contract, ((), ())), preferred_element_type=F32)


def iota(shape, axis):
    return lax.broadcasted_iota(jnp.int32, shape, axis)


def top_half(shape, rows):
    return iota(shape, 0) % (2 * rows) < rows


def spread(value, rows):
    count, dim = value.shape
    left, right = value[:, : dim // 2], value[:, dim // 2 :]
    top = top_half(left.shape, rows)
    even = jnp.where(top, left, pltpu.roll(right, rows, 0))
    odd = jnp.where(top, pltpu.roll(left, count - rows, 0), right)
    shape = (count // (2 * rows), 2 * rows, dim // 2)
    return even.reshape(shape), odd.reshape(shape)


def unspread(even, odd, rows):
    shape = (even.shape[0] * 2 * rows, even.shape[2])
    even, odd = even.reshape(shape), odd.reshape(shape)
    top = top_half(shape, rows)
    left = jnp.where(top, even, pltpu.roll(odd, rows, 0))
    right = jnp.where(top, pltpu.roll(even, shape[0] - rows, 0), odd)
    return jnp.concatenate([left, right], axis=1)


def kernel(
    clips,
    shards,
    tokens,
    scales,
    slot_params,
    w1,
    b1,
    w2,
    b2,
    combine,
    returned,
    feat,
    scale_v,
    params_v,
    w1_v,
    b1_v,
    w2_v,
    b2_v,
    logits,
    lifted,
    combine_v,
    stats,
    lifted_v,
    partial_out,
    sums,
    back_out,
    back_in,
    local_sem,
    token_sem,
    send_a,
    recv_a,
    send_b,
    recv_b,
    send_c,
    recv_c,
):
    c_me, s_me = lax.axis_index("clip"), lax.axis_index("shard")
    count, dim = feat.shape
    blocks = scale_v.shape[0]
    width = dim // blocks
    slots = params_v.shape[1]
    experts, _, ff = w1_v.shape
    rows = slots // (clips * shards)
    each = rows // experts
    group = clips * rows
    devices = clips * shards
    me = c_me * shards + s_me
    chunks = count // CHUNK

    def span(i):
        return pl.ds(i * CHUNK, CHUNK)

    load_scale = pltpu.make_async_copy(scales, scale_v, local_sem.at[0])
    load_params = pltpu.make_async_copy(slot_params, params_v, local_sem.at[1])
    load_params.start()
    load_scale.start()
    for i in range(chunks):
        pltpu.make_async_copy(
            tokens.at[pl.ds(i * CHUNK, CHUNK)], feat.at[pl.ds(i * CHUNK, CHUNK)], token_sem.at[i]
        ).start()
    weight_loads = [
        pltpu.make_async_copy(w1, w1_v, local_sem.at[2]),
        pltpu.make_async_copy(b1, b1_v, local_sem.at[3]),
        pltpu.make_async_copy(w2, w2_v, local_sem.at[4]),
        pltpu.make_async_copy(b2, b2_v, local_sem.at[5]),
    ]
    for load in weight_loads:
        load.start()

    barrier = pltpu.get_barrier_semaphore()

    def place(d):
        at = lax.rem(me + d, devices)
        return at, at // shards, lax.rem(at, shards)

    def greet(d, carry):
        _, c, s = place(d)
        pl.semaphore_signal(barrier, inc=1, device_id=(c, s), device_id_type=MESH)
        return carry

    lax.fori_loop(1, devices, greet, 0)
    load_params.wait()
    load_scale.wait()

    peak = jnp.full((1, slots), -jnp.inf, F32)
    for i in range(chunks):
        at = span(i)
        pltpu.make_async_copy(tokens.at[at], feat.at[at], token_sem.at[i]).wait()
        scale = scale_v[:, 0, at].T
        scaled = jnp.concatenate(
            [
                feat[at, b * width : (b + 1) * width].astype(F32) * scale[:, b : b + 1]
                for b in range(blocks)
            ],
            axis=1,
        ).astype(BF16)
        feat[at, :] = scaled
        value = dot(scaled, params_v[...])
        logits[at, :] = value
        peak = jnp.maximum(peak, jnp.max(value, axis=0, keepdims=True))

    total = jnp.zeros((1, slots), F32)
    for i in range(chunks):
        at = span(i)
        value = jnp.exp(logits[at, :] - peak)
        lifted[at, :] = value
        total = total + jnp.sum(value, axis=0, keepdims=True)
    which = iota((8, slots), 0)
    stats[s_me] = jnp.where(which == 0, peak, total)

    pl.semaphore_wait(barrier, devices - 1)

    def shard_copies(make):
        return [make(d, lax.rem(s_me + d, shards)) for d in range(1, shards)]

    stats_sent = shard_copies(
        lambda d, to: pltpu.make_async_remote_copy(
            src_ref=stats.at[s_me],
            dst_ref=stats.at[s_me],
            send_sem=send_a.at[d],
            recv_sem=recv_a.at[s_me],
            device_id=(c_me, to),
            device_id_type=MESH,
        )
    )
    for copy in stats_sent:
        copy.start()

    for d in range(1, shards):
        origin = lax.rem(s_me + d, shards)
        pltpu.make_async_copy(stats.at[origin], stats.at[origin], recv_a.at[origin]).wait()
    top = stats[0, 0:1, :]
    for s in range(1, shards):
        top = jnp.maximum(top, stats[s, 0:1, :])
    total = jnp.zeros((1, slots), F32)
    for s in range(shards):
        total = total + stats[s, 1:2, :] * jnp.exp(stats[s, 0:1, :] - top)

    lift = jnp.exp(peak - top) / total
    for i in range(chunks):
        at = span(i)
        lifted_v[at, :] = (lifted[at, :] * lift).astype(BF16)
    partial = dot(lifted_v[...], feat[...], ((0,), (0,)))
    even, odd = spread(partial, rows)
    partial_out[:, 0] = even
    partial_out[:, 1] = odd

    def send_sum(d):
        to, c, s = place(d)
        return pltpu.make_async_remote_copy(
            src_ref=partial_out.at[to // 2, lax.rem(to, 2)],
            dst_ref=sums.at[s_me, c_me // 2, lax.rem(c_me, 2)],
            send_sem=send_b.at[d],
            recv_sem=recv_b.at[me],
            device_id=(c, s),
            device_id_type=MESH,
        )

    def start_sum(d, carry):
        send_sum(d).start()
        return carry

    lax.fori_loop(1, devices, start_sum, 0)
    sums[s_me, c_me // 2, lax.rem(c_me, 2)] = partial_out[me // 2, lax.rem(me, 2)]

    for i in range(chunks):
        at = span(i)
        value = logits[at, :]
        weights = jnp.exp(value - jnp.max(value, axis=1, keepdims=True))
        combine_v[at, :] = (weights / jnp.sum(weights, axis=1, keepdims=True)).astype(BF16)
    store = pltpu.make_async_copy(combine_v, combine, local_sem.at[6])
    store.start()

    def await_sum(d, carry):
        origin, c, s = place(d)
        landed = sums.at[s, c // 2, lax.rem(c, 2)]
        pltpu.make_async_copy(landed, landed, recv_b.at[origin]).wait()
        return carry

    lax.fori_loop(1, devices, await_sum, 0)
    value = sums[0]
    for s in range(1, shards):
        value = value + sums[s]
    wide = unspread(value[:, 0], value[:, 1], rows).astype(BF16).astype(F32)

    mean = jnp.mean(wide * wide, axis=-1, keepdims=True)
    normalized = (wide * lax.rsqrt(mean + 1e-06)).astype(BF16)
    for load in weight_loads:
        load.wait()

    def mine(shape, expert):
        return (iota(shape, 0) % rows) // each == expert

    def choose(values):
        chosen = values[0]
        for e in range(1, experts):
            chosen = jnp.where(mine(chosen.shape, e), values[e], chosen)
        return chosen

    def spread_bias(ref, at):
        value = ref[:, at].astype(F32)
        size = (group, value.shape[1])
        return choose([jnp.broadcast_to(value[e : e + 1], size) for e in range(experts)])

    def expert_step(f, outs):
        at = pl.ds(pl.multiple_of(f * HIDDEN_CHUNK, HIDDEN_CHUNK), HIDDEN_CHUNK)
        before = choose([dot(normalized, w1_v[e, :, at]) for e in range(experts)])
        before = before + spread_bias(b1_v, at)
        hidden = (0.5 * before * (1.0 + lax.erf(before * math.sqrt(0.5)))).astype(BF16)
        return tuple(outs[e] + dot(hidden, w2_v[e, at, :]) for e in range(experts))

    outs = tuple(jnp.zeros((group, dim), F32) for _ in range(experts))
    outs = lax.fori_loop(0, ff // HIDDEN_CHUNK, expert_step, outs, unroll=True)
    result = (choose(outs) + spread_bias(b2_v, slice(None))).astype(BF16).astype(F32)
    even, odd = spread(result, rows)
    back_out[:, 0] = even.astype(BF16)
    back_out[:, 1] = odd.astype(BF16)

    def send_back(d):
        to, c, s = place(d)
        return pltpu.make_async_remote_copy(
            src_ref=back_out.at[c // 2, lax.rem(c, 2)],
            dst_ref=back_in.at[me // 2, lax.rem(me, 2)],
            send_sem=send_c.at[d],
            recv_sem=recv_c.at[me],
            device_id=(c, s),
            device_id_type=MESH,
        )

    def start_back(d, carry):
        send_back(d).start()
        return carry

    lax.fori_loop(1, devices, start_back, 0)
    back_in[me // 2, lax.rem(me, 2)] = back_out[c_me // 2, lax.rem(c_me, 2)]
    for copy in stats_sent:
        copy.wait_send()
    store.wait()

    def await_back(d, carry):
        origin, c, s = place(d)
        landed = back_in.at[origin // 2, lax.rem(origin, 2)]
        pltpu.make_async_copy(landed, landed, recv_c.at[origin]).wait()
        return carry

    lax.fori_loop(1, devices, await_back, 0)
    value = back_in[...].astype(F32)
    returned[...] = unspread(value[:, 0], value[:, 1], rows).astype(BF16)

    def finish(d, carry):
        send_sum(d).wait_send()
        send_back(d).wait_send()
        return carry

    lax.fori_loop(1, devices, finish, 0)


def local(clips, shards, tokens, scales, slot_params, w1, b1, w2, b2):
    count, dim = tokens.shape[1:]
    blocks = scales.shape[1]
    slots = slot_params.shape[1]
    rows = slots // (clips * shards)
    devices = clips * shards
    piece = (2, 2 * rows, dim // 2)
    combine, returned = pl.pallas_call(
        functools.partial(kernel, clips, shards),
        out_shape=(
            jax.ShapeDtypeStruct((count, slots), BF16),
            jax.ShapeDtypeStruct((slots, dim), BF16),
        ),
        in_specs=[pl.BlockSpec(memory_space=pl.ANY)] * 7,
        out_specs=(pl.BlockSpec(memory_space=pl.ANY), pl.BlockSpec(memory_space=pltpu.VMEM)),
        scratch_shapes=[
            pltpu.VMEM((count, dim), BF16),
            pltpu.VMEM((blocks, 1, count), F32),
            pltpu.VMEM(slot_params.shape, BF16),
            pltpu.VMEM(w1.shape, BF16),
            pltpu.VMEM(b1.shape, BF16),
            pltpu.VMEM(w2.shape, BF16),
            pltpu.VMEM(b2.shape, BF16),
            pltpu.VMEM((count, slots), F32),
            pltpu.VMEM((count, slots), F32),
            pltpu.VMEM((count, slots), BF16),
            pltpu.VMEM((shards, 8, slots), F32),
            pltpu.VMEM((count, slots), BF16),
            pltpu.VMEM((devices // 2,) + piece, F32),
            pltpu.VMEM((shards, clips // 2) + piece, F32),
            pltpu.VMEM((clips // 2,) + piece, BF16),
            pltpu.VMEM((devices // 2,) + piece, BF16),
            pltpu.SemaphoreType.DMA((7,)),
            pltpu.SemaphoreType.DMA((count // CHUNK,)),
            pltpu.SemaphoreType.DMA((shards,)),
            pltpu.SemaphoreType.DMA((shards,)),
            pltpu.SemaphoreType.DMA((devices,)),
            pltpu.SemaphoreType.DMA((devices,)),
            pltpu.SemaphoreType.DMA((devices,)),
            pltpu.SemaphoreType.DMA((devices,)),
        ],
        compiler_params=pltpu.CompilerParams(
            collective_id=0, has_side_effects=True, vmem_limit_bytes=56 << 20
        ),
        name="slots",
    )(tokens[0], scales.transpose(1, 0, 2), slot_params, w1, b1, w2, b2)
    mixed = jnp.dot(combine, returned, preferred_element_type=F32).astype(BF16)
    return mixed[None]


def solution(mesh):
    placed = (
        P("clip", "shard", None),
        P("clip", None, "shard"),
        P(),
        P(("clip", "shard"), None, None),
        P(("clip", "shard"), None),
        P(("clip", "shard"), None, None),
        P(("clip", "shard"), None),
    )
    return jax.shard_map(
        functools.partial(local, mesh.shape["clip"], mesh.shape["shard"]),
        mesh=mesh,
        in_specs=placed,
        out_specs=P("clip", "shard", None),
        check_vma=False,
    )
```
